256 devices in a mesh: seq: 32 (over z, y), exp: 8 (over x, core).
Axes of the slice: x: 4, y: 4, z: 8, core: 2. Of those that a mesh axis runs over, the one named last changes fastest.
Arguments:
- residual: bfloat16 [4096, 6144], P('exp', 'seq'), may hold values from -8 to 8
- query: bfloat16 [4096, 8192], P('seq', 'exp'), may hold values from -6 to 6
- key_in: bfloat16 [4096, 8192], P('seq', 'exp'), may hold values from -6 to 6
- value_in: bfloat16 [4096, 8192], P('seq', 'exp'), may hold values from -0.75 to 0.75
- gate_in: bfloat16 [4096, 8192], P('seq', 'exp'), may hold values from -6 to 6
- log_decay: float32 [4096, 64], P('seq', 'exp'), may hold values from -2 to 0
- state_in: float32 [64, 128, 128], P('exp'), may hold values from -12 to 12
- attn_gain: float32 [8192], P('exp'), may hold values from 0.1 to 1.9
- w_out: bfloat16 [8192, 6144], P('exp', 'seq'), may hold values from -0.0625 to 0.0625
- moe_gain: float32 [6144], P('seq'), may hold values from 0.1 to 1.9
- router: float32 [6144, 32], P('seq'), may hold values from -0.078125 to 0.078125
- w_gate: bfloat16 [8, 9216, 6144], P('exp', 'seq'), may hold values from -0.078125 to 0.078125
- w_up: bfloat16 [8, 9216, 6144], P('exp', 'seq'), may hold values from -0.078125 to 0.078125
- w_down: bfloat16 [8, 9216, 6144], P('exp', None, 'seq'), may hold values from -0.125 to 0.125
- expert_ids: int32 [4096, 2], P('exp'), may hold values from 0 to 31, all different within a row; in each aligned block of 512 rows (0 to 511, 512 to 1023, ...) at most 40 rows name the same one
- keep_counts: int32 [32], replicated, may hold values from 64 to 319
Outputs:
- layer_out: bfloat16 [4096, 6144], P('exp', 'seq')
- final_state: float32 [64, 128, 128], P('exp', 'seq')
The draws below stay inside these ranges and needn't reach their ends.
Inputs may be any that keep to these rules, and one draw needn't show every extreme that they name: `expert_ids`: each row names 2 different experts. Among the rows of one device no expert is named more than 40 times, a bound that some block reaches.
All inputs are finite; a program needn't handle non-finite values.
Results may differ from the reference program's by a relative error of at most 0.014.
Values may be sent and summed in bfloat16 or wider, within the bound.
A program may use at most 128 MiB of HBM per device.

```python
import math
import jax
import jax.numpy as jnp
import numpy as np
from jax import lax

D = 6144
HEAD_TOTAL = 64
HD = 128
FF = 9216
EXPERTS = 32
TOP = 2
TOK_DEV = 128
TOKEN_TOTAL = 4096
BLOCK = 512
WINDOW = 8
CAP = 40
N_EXP = 8


def draw_residual(key, part):
    random_subkeys = jax.random.split(key, 3)
    column_pos = jnp.arange(D, dtype=jnp.float32) / D
    column_scale = jnp.exp(column_pos * math.log(3.0)) * jnp.exp(jax.random.uniform(random_subkeys[1], (D,), jnp.float32, -0.6, 0.6))
    base_draw = jax.random.normal(random_subkeys[0], (TOKEN_TOTAL, D), jnp.float32)
    row_scale = jnp.exp(jax.random.uniform(random_subkeys[2], (TOKEN_TOTAL, 1), jnp.float32, -0.35, 0.35))
    values = base_draw * row_scale
    return jnp.clip(values * column_scale * 0.4, -8.0, 8.0).astype(jnp.bfloat16)


def draw_log_decay(key, part):
    random_subkeys = jax.random.split(key, 7)
    is_fast = jax.random.bernoulli(random_subkeys[0], 0.5, (1, HEAD_TOTAL))
    slow_rate = jnp.exp(jax.random.uniform(random_subkeys[1], (1, HEAD_TOTAL), jnp.float32, math.log(0.03), math.log(0.3))) / TOKEN_TOTAL
    fast_rate = jax.random.uniform(random_subkeys[2], (1, HEAD_TOTAL), jnp.float32, 1.0 / 50.0, 1.0 / 30.0)
    baseline_decay_rate = jnp.where(is_fast, fast_rate, slow_rate)
    blocks = TOKEN_TOTAL // TOK_DEV
    block_multiplier = jnp.exp(jax.random.uniform(random_subkeys[3], (blocks, 1, HEAD_TOTAL), jnp.float32, -math.log(2.0), math.log(2.0)))
    block_multiplier = jnp.broadcast_to(block_multiplier, (blocks, TOK_DEV, HEAD_TOTAL)).reshape(TOKEN_TOTAL, HEAD_TOTAL)
    random_perturbation = jnp.exp(jax.random.uniform(random_subkeys[4], (TOKEN_TOTAL, HEAD_TOTAL), jnp.float32, -math.log(1.4), math.log(1.4)))
    spike_positions = jax.random.randint(random_subkeys[5], (2, HEAD_TOTAL), 0, TOKEN_TOTAL)
    spike_strength = jax.random.uniform(random_subkeys[6], (2, HEAD_TOTAL), jnp.float32, math.log(0.5), math.log(0.8))
    spike_flags = (jnp.arange(TOKEN_TOTAL)[:, None, None] == spike_positions[None, :, :]).astype(jnp.float32)
    spike_events = jnp.sum(spike_flags * spike_strength[None], axis=1)
    return -baseline_decay_rate * block_multiplier * random_perturbation + spike_events


def place_ends(drawn, own_key, smallest, largest):
    spot = [jax.random.randint(jax.random.fold_in(own_key, axis), (), 0, length) for axis, length in enumerate(drawn.shape)]
    longest = drawn.shape.index(max(drawn.shape))
    next_to = spot[:longest] + [(spot[longest] + 1) % drawn.shape[longest]] + spot[longest + 1:]
    return drawn.at[tuple(spot)].set(smallest).at[tuple(next_to)].set(largest)


def spiked(array, stream_key, source, target, shards_of, factor):
    def block_of(position):
        return (jnp.arange(array.shape[position]) // (array.shape[position] // shards_of)).reshape((-1,) + (1,) * (array.ndim - 1 - position))

    near = jax.random.permutation(stream_key, shards_of)[block_of(target)]
    far = (block_of(target) + shards_of // 2) % shards_of
    return jnp.where((block_of(source) == near) | (block_of(source) == far), factor * array, array)


def shard_levels(rng, dims, pieces, low, largest):
    loudness = 1.0
    for axis_at, blocks in pieces:
        steps = jax.random.uniform(jax.random.fold_in(jax.random.fold_in(rng, 6), axis_at), (blocks,), jnp.float32, low / len(pieces), largest / len(pieces))
        loudness = loudness * jnp.repeat(jnp.exp(steps), dims[axis_at] // blocks).reshape((-1,) + (1,) * (len(dims) - 1 - axis_at))
    return loudness


def deal_out(stream_key, own, number, rows, number_of, top, reach, lean):
    ranking = jax.random.permutation(stream_key, number_of)
    packed, ordinary = portions_of(number_of, rows * top, reach, lean, True), portions_of(number_of, rows * top, reach, lean, False)
    places = jnp.arange(number_of)

    def named(sizes, turn):
        used = int((sizes > 0).sum())
        fixed = max(1, used // 4)
        moved = fixed + (places - fixed + turn * (used - fixed)) % max(1, number_of - fixed)
        return jnp.zeros((number_of,), jnp.int32).at[ranking[jnp.where(places < fixed, places, moved)]].set(jnp.asarray(sizes, jnp.int32))

    sizes = jnp.where(number % 4 == 0, named(packed, number // 4), named(ordinary, number - number // 4 - 1))
    mixed = jax.random.permutation(jax.random.fold_in(own, 3), number_of)
    donor, taker = mixed[0:number_of // 2 * 2:2], mixed[1:number_of // 2 * 2:2]
    slack = jnp.minimum(sizes[donor] - 1, reach - sizes[taker]) // 2
    slack = jnp.where((donor == ranking[0]) | (taker == ranking[0]) | (sizes[taker] == 0), 0, jnp.maximum(slack, 0))
    moved = jax.random.randint(jax.random.fold_in(own, 4), (number_of // 2,), 0, 1 << 20) % (slack + 1)
    sizes = sizes.at[donor].add(-moved).at[taker].add(moved)
    labels = jnp.searchsorted(jnp.cumsum(sizes), jnp.arange(rows * top), side="right").astype(jnp.int32)
    listing = labels.reshape(top, rows).T
    listing = listing[jax.random.permutation(jax.random.fold_in(own, 1), rows)]
    turn = jax.random.randint(jax.random.fold_in(own, 2), (rows, 1), 0, top)
    return jnp.take_along_axis(listing, (jnp.arange(top)[None, :] + turn) % top, axis=1)


def portions_of(amount, total, bound, lean, full):
    weights = [(1 << 20) // math.isqrt(grade ** lean) + 1 for grade in range(1, amount + 1)]
    largest = bound if full else min(bound, max(-(-total // amount), total * weights[0] // sum(weights)))
    least = 1 if total - largest >= amount - 1 else 0
    given, spare = [largest] + [least] * (amount - 1), total - largest - least * (amount - 1)
    while spare > 0:
        candidates = [i for i in range(1, amount) if given[i] < largest] or [i for i in range(1, amount) if given[i] < bound]
        mass, remaining = sum([weights[i] for i in candidates]), spare
        for i in candidates:
            addition = min(bound - given[i], max(1, remaining * weights[i] // mass), spare)
            given[i] = given[i] + addition
            spare = spare - addition
    return np.array(given)


def gaussian(key, dims, deviation, bound, cuts=(), kind=jnp.bfloat16):
    values = deviation * jax.random.normal(key, dims, jnp.float32)
    if cuts:
        values = values * shard_levels(key, dims, cuts, -0.22, 0.18)
    return jnp.clip(values, -bound, bound).astype(kind)


def bell_draw_with(rng, dims, scale, bound, shards, heavy, held_as=jnp.bfloat16):
    result = scale * jax.random.normal(rng, dims, jnp.float32)
    if shards:
        result = result * shard_levels(rng, dims, shards, -0.22, 0.18)
    return jnp.clip(spiked(result, jax.random.fold_in(rng, 3), *heavy), -bound, bound).astype(held_as)


def setup_inputs(seed: int = 0) -> dict:
    seeds = jax.random.split(jax.random.key(seed), 17)
    residual = draw_residual(jax.random.fold_in(seeds[16], 71), 0)
    query = gaussian(seeds[1], (TOKEN_TOTAL, HEAD_TOTAL * HD), 1.0, 6.0, ((0, 32), (1, 8)))
    key_in = gaussian(seeds[2], (TOKEN_TOTAL, HEAD_TOTAL * HD), 1.0, 6.0, ((0, 32), (1, 8)))
    value_in = gaussian(seeds[3], (TOKEN_TOTAL, HEAD_TOTAL * HD), 0.125, 0.75, ((0, 32), (1, 8)))
    gate_in = gaussian(seeds[4], (TOKEN_TOTAL, HEAD_TOTAL * HD), 1.0, 6.0, ((0, 32), (1, 8)))
    log_decay = draw_log_decay(jax.random.fold_in(seeds[16], 71), 0)
    state_in = gaussian(seeds[6], (HEAD_TOTAL, HD, HD), 2.0, 12.0, ((0, 8),), jnp.float32)
    attn_gain = jnp.clip(1.0 + 0.18 * jax.random.normal(seeds[7], (HEAD_TOTAL * HD,), jnp.float32), 0.1, 1.9)
    w_out = gaussian(seeds[8], (HEAD_TOTAL * HD, D), (HEAD_TOTAL * HD) ** -0.5, 0.0625, ((0, 8), (1, 32)))
    moe_gain = jnp.clip(1.0 + 0.18 * jax.random.normal(seeds[9], (D,), jnp.float32), 0.1, 1.9)
    router = gaussian(seeds[10], (D, EXPERTS), D ** -0.5, 0.078125, ((0, 32),), jnp.float32)
    w_gate = gaussian(seeds[11], (WINDOW, FF, D), D ** -0.5, 0.078125, ((0, 8), (1, 32)))
    w_up = gaussian(seeds[12], (WINDOW, FF, D), D ** -0.5, 0.078125, ((0, 8), (1, 32)))
    w_down = bell_draw_with(seeds[13], (WINDOW, FF, D), FF ** -0.5, 0.125, ((0, 8), (2, 32)), (1, 2, 32, 2.75))
    expert_ids_keys = jax.random.split(jax.random.fold_in(seeds[14], 1), TOKEN_TOTAL // BLOCK)
    expert_ids_turns = jax.random.permutation(jax.random.fold_in(seeds[14], 3), TOKEN_TOTAL // BLOCK)
    expert_ids = jax.vmap(lambda own, number: deal_out(jax.random.fold_in(seeds[14], 2), own, number, BLOCK, EXPERTS, TOP, CAP, 1))(expert_ids_keys, expert_ids_turns).reshape((TOKEN_TOTAL, TOP))
    keep_counts = place_ends(jax.random.randint(seeds[15], (EXPERTS,), TOKEN_TOTAL * TOP // (4 * EXPERTS), 5 * TOKEN_TOTAL * TOP // (4 * EXPERTS)), jax.random.fold_in(seeds[15], 1), TOKEN_TOTAL * TOP // (4 * EXPERTS), (5 * TOKEN_TOTAL * TOP // (4 * EXPERTS)) - 1).astype(jnp.int32)
    return dict(residual=residual, query=query, key_in=key_in, value_in=value_in, gate_in=gate_in, log_decay=log_decay, state_in=state_in, attn_gain=attn_gain, w_out=w_out, moe_gain=moe_gain, router=router, w_gate=w_gate, w_up=w_up, w_down=w_down, expert_ids=expert_ids, keep_counts=keep_counts)


epsilon = 1e-05
highest = lax.Precision.HIGHEST

def block_terms(act_query, act_key, val_rows, log_rows):
    running_log = jnp.cumsum(log_rows, axis=0)
    block_log = running_log[-1]
    length = log_rows.shape[0]
    causal_mask = (jnp.arange(length)[:, None] >= jnp.arange(length)[None, :])[None]
    flipped = jnp.transpose(running_log)
    log_gap = flipped[:, :, None] - flipped[:, None, :]
    decay_rows = jnp.where(causal_mask, jnp.exp(jnp.where(causal_mask, log_gap, 0.0)), 0.0)
    scores = jnp.einsum('thd,shd->hts', act_query, act_key, precision=highest)
    local_part = jnp.einsum('hts,shd->thd', scores * decay_rows, val_rows, precision=highest)
    tail_decay = jnp.exp(block_log[None, :] - running_log)
    update = jnp.einsum('shd,she->hde', act_key * tail_decay[:, :, None], val_rows, precision=highest)
    return (local_part, running_log, block_log, update)

def from_state(act_query, running_log, state_carry):
    return jnp.einsum('thd,hde->the', act_query * jnp.exp(running_log)[:, :, None], state_carry, precision=highest)

def reference(residual, query, key_in, value_in, gate_in, log_decay, state_in, attn_gain, w_out, moe_gain, router, w_gate, w_up, w_down, expert_ids, keep_counts):
    act_query = jax.nn.silu(query.astype(jnp.float32)).reshape(TOKEN_TOTAL, HEAD_TOTAL, HD)
    act_key = jax.nn.silu(key_in.astype(jnp.float32)).reshape(TOKEN_TOTAL, HEAD_TOTAL, HD)
    val_rows = value_in.astype(jnp.float32).reshape(TOKEN_TOTAL, HEAD_TOTAL, HD)
    blocks = TOKEN_TOTAL // TOK_DEV

    def block_step(state_carry, portions):
        query_block, key_block, value_block, log_block = portions
        local_part, running_log, block_log, update = block_terms(query_block, key_block, value_block, log_block)
        outputs = local_part + from_state(query_block, running_log, state_carry)
        state_next = jnp.exp(block_log)[:, None, None] * state_carry + update
        return (state_next, outputs)
    last_state, outputs = lax.scan(block_step, state_in, (act_query.reshape(blocks, TOK_DEV, HEAD_TOTAL, HD), act_key.reshape(blocks, TOK_DEV, HEAD_TOTAL, HD), val_rows.reshape(blocks, TOK_DEV, HEAD_TOTAL, HD), log_decay.reshape(blocks, TOK_DEV, HEAD_TOTAL)))
    outputs = outputs.reshape(TOKEN_TOTAL, HEAD_TOTAL, HD)
    square_mean = lax.optimization_barrier(jnp.mean(outputs * outputs, axis=2, keepdims=True))
    normed = outputs * lax.rsqrt(square_mean + epsilon) * attn_gain.reshape(HEAD_TOTAL, HD)
    heads_mixed = (normed.reshape(TOKEN_TOTAL, HEAD_TOTAL * HD) * jax.nn.sigmoid(gate_in.astype(jnp.float32))).astype(jnp.bfloat16)
    after_attn = residual.astype(jnp.float32) + jnp.dot(heads_mixed, w_out, preferred_element_type=jnp.float32)
    model_mean = lax.optimization_barrier(jnp.mean(after_attn * after_attn, axis=1, keepdims=True))
    scaled = after_attn * lax.rsqrt(model_mean + epsilon) * moe_gain
    routed_in = scaled.astype(jnp.bfloat16)
    logits = jnp.dot(scaled, router, precision=highest)
    chosen = jnp.take_along_axis(logits, expert_ids, axis=1)
    gate_probs = jnp.stack([jax.nn.sigmoid(chosen[:, 0] - chosen[:, 1]), jax.nn.sigmoid(chosen[:, 1] - chosen[:, 0])], axis=1)
    flat_ids = expert_ids.reshape(TOKEN_TOTAL * TOP)
    onehot = (flat_ids[:, None] == jnp.arange(WINDOW, dtype=jnp.int32)[None, :]).astype(jnp.int32)
    global_rank = lax.optimization_barrier(jnp.sum((jnp.cumsum(onehot, axis=0) - onehot) * onehot, axis=1)).astype(jnp.int32)
    grouped = onehot.reshape(N_EXP, BLOCK * TOP, WINDOW)
    local_rank = lax.optimization_barrier(jnp.sum(((jnp.cumsum(grouped, axis=1) - grouped) * grouped).reshape(TOKEN_TOTAL * TOP, WINDOW), axis=1)).astype(jnp.int32)
    in_window = flat_ids < WINDOW
    safe_ids = jnp.where(in_window, flat_ids, 0).astype(jnp.int32)
    is_kept = in_window & (global_rank < keep_counts[safe_ids])
    order = jnp.arange(TOKEN_TOTAL * TOP, dtype=jnp.int32)
    slot_index = (order // (BLOCK * TOP) * CAP + local_rank).astype(jnp.int32)
    target = jnp.where(in_window, flat_ids, WINDOW).astype(jnp.int32)
    slot_tokens = jnp.zeros((WINDOW, N_EXP * CAP), jnp.int32).at[target, slot_index].set((order // TOP).astype(jnp.int32), mode='drop')

    def expert(portions):
        gate_rows, up_rows, down_rows, token_rows = portions
        chosen_rows = routed_in[token_rows]
        gate_val = jnp.dot(chosen_rows, gate_rows.T, preferred_element_type=jnp.float32)
        up_val = jnp.dot(chosen_rows, up_rows.T, preferred_element_type=jnp.float32)
        hidden = (jax.nn.silu(gate_val) * up_val).astype(jnp.bfloat16)
        return jnp.dot(hidden, down_rows, preferred_element_type=jnp.float32).astype(jnp.bfloat16)
    expert_out = lax.map(expert, (w_gate, w_up, w_down, slot_tokens))
    flat_out = expert_out.reshape(WINDOW * N_EXP * CAP, D)
    flat_index = jnp.where(is_kept, safe_ids * (N_EXP * CAP) + slot_index, 0).astype(jnp.int32)
    picked = flat_out[flat_index].astype(jnp.float32).reshape(TOKEN_TOTAL, TOP, D)
    weight = jnp.where(is_kept.reshape(TOKEN_TOTAL, TOP), gate_probs, 0.0)
    expert_sum = lax.optimization_barrier(jnp.sum(picked * weight[:, :, None], axis=1))
    return ((after_attn + expert_sum).astype(jnp.bfloat16), last_state)
```

```python
import jax
import jax.numpy as jnp
from jax import lax
from jax.experimental import pallas as pl
from jax.experimental.pallas import tpu as pltpu
from jax.sharding import PartitionSpec as P

f32, bf16 = jnp.float32, jnp.bfloat16
highest = lax.Precision.HIGHEST
epsilon = 1e-05
D = 6144
NS, NE, NY, NZ = 32, 8, 4, 8
HEADS, HD, TOK = 8, 128, 128
COLS = 192
MESH = pl.DeviceIdType.MESH


def silu(v):
    return v / (1.0 + jnp.exp(-v))


def iota(shape, dim):
    return lax.broadcasted_iota(jnp.int32, shape, dim)


def remote(src, dst, send, recv, dev):
    return pltpu.make_async_remote_copy(
        src_ref=src, dst_ref=dst, send_sem=send, recv_sem=recv, device_id=dev, device_id_type=MESH
    )


def enter(s, e):
    barrier = pltpu.get_barrier_semaphore()

    def seq_signal(o, _):
        pl.semaphore_signal(
            barrier, inc=1, device_id=(lax.rem(s + o, NS), e), device_id_type=MESH
        )
        return 0

    def exp_signal(o, _):
        pl.semaphore_signal(
            barrier, inc=1, device_id=(s, lax.rem(e + o, NE)), device_id_type=MESH
        )
        return 0

    lax.fori_loop(1, NS, seq_signal, 0)
    lax.fori_loop(1, NE, exp_signal, 0)
    return barrier


def attention_kernel(
    q_ref, k_ref, v_ref, g_ref, ld_ref, st_ref, gain_ref, w_hbm, res_ref,
    after_ref, fin_ref,
    ldp, lcol, lrow, kbf, upd, ub, rbuf, pref, pbuf, inc, loc, qd,
    wbuf, wcat, act, pb, sb, qb, rs, ysend, yrecv,
    w_local, w_send, w_recv, a_send, a_recv, b_send, b_recv,
    r_send, r_recv, sb_send, sb_recv, rs_send, rs_recv, y_send, y_recv,
):
    s = lax.axis_index("seq")
    e = lax.axis_index("exp")
    y, z = lax.rem(s, NY), s // NY
    c = lax.rem(e, 2)
    barrier = enter(s, e)
    wl = pltpu.make_async_copy(w_hbm, wbuf.at[y], w_local)
    wl.start()

    ldp[...] = jnp.zeros_like(ldp)
    ldp[:, 0:HEADS] = ld_ref[...]
    tri = (iota((TOK, TOK), 0) >= iota((TOK, TOK), 1)).astype(f32)
    run = jnp.dot(tri, ldp[...], preferred_element_type=f32, precision=highest)
    lcol[...] = run
    lrow[...] = run.T
    for h in range(HEADS):
        cols = slice(h * HD, (h + 1) * HD)
        kh = silu(k_ref[:, cols].astype(f32))
        kbf[:, cols] = kh.astype(bf16)
        tail = jnp.exp(lcol[TOK - 1 : TOK, h : h + 1] - lcol[:, h : h + 1])
        kd = (kh * tail).T.astype(bf16)
        upd[cols, :] = jnp.dot(kd, v_ref[:, cols], preferred_element_type=f32)
    total = jnp.broadcast_to(lrow[0:HEADS, TOK - 1 : TOK], (HEADS, HD))
    high = total.astype(bf16).astype(f32)
    logs = jnp.concatenate([high, total - high], axis=0).astype(bf16)
    for d in range(NS):
        rows = [upd[pl.ds(4 * d + r, HEADS, stride=HD), :] for r in range(4)]
        ub[d, 0:32, :] = jnp.concatenate(rows, axis=0).astype(bf16)
        ub[d, 32:48, :] = logs

    pl.semaphore_wait(barrier, NS - 1 + NE - 1)

    def send_a(o, _):
        peer = lax.rem(s + o, NS)
        remote(ub.at[peer], rbuf.at[s], a_send.at[o], a_recv.at[s], (peer, e)).start()
        return 0

    lax.fori_loop(1, NS, send_a, 0)
    rbuf[s] = ub[s]
    y_right, y_left = lax.rem(y + 1, NY), lax.rem(y + NY - 1, NY)
    y_far = lax.rem(y + 2, NY)
    dev_yr, dev_yl = (z * NY + y_right, e), (z * NY + y_left, e)
    w_r = remote(w_hbm, wbuf.at[y], w_send.at[0], w_recv.at[0], dev_yr)
    w_l = remote(w_hbm, wbuf.at[y], w_send.at[1], w_recv.at[1], dev_yl)
    w_r.start()
    w_l.start()

    causal = iota((TOK, TOK), 0) >= iota((TOK, TOK), 1)
    for h in range(HEADS):
        cols = slice(h * HD, (h + 1) * HD)
        qh = silu(q_ref[:, cols].astype(f32))
        lc = lcol[:, h : h + 1]
        gap = lc - lrow[h : h + 1, :]
        decay = jnp.where(causal, jnp.exp(jnp.where(causal, gap, 0.0)), 0.0)
        scores = lax.dot_general(
            qh.astype(bf16), kbf[:, cols], (((1,), (1,)), ((), ())), preferred_element_type=f32
        )
        loc[:, cols] = jnp.dot(
            (scores * decay).astype(bf16), v_ref[:, cols], preferred_element_type=f32
        )
        qd[:, cols] = (qh * jnp.exp(lc)).astype(bf16)

    def wait_a(o, _):
        src = lax.rem(s + o, NS)
        remote(rbuf.at[src], rbuf.at[src], a_send.at[o], a_recv.at[src], (src, e)).wait_recv()
        return 0

    lax.fori_loop(1, NS, wait_a, 0)
    start = jnp.concatenate(
        [st_ref[pl.ds(4 * s + r, HEADS, stride=HD), :] for r in range(4)], axis=0
    )

    def scan(j, state):
        pref[j] = state.astype(bf16)
        piece = rbuf[j].astype(f32)
        dec = jnp.exp(piece[32:40] + piece[40:48])
        return state * jnp.concatenate([dec] * 4, axis=0) + piece[0:32]

    last = lax.fori_loop(0, NS, scan, start)
    for r in range(4):
        for h in range(HEADS):
            fin_ref[h, r : r + 1, :] = last[8 * r + h : 8 * r + h + 1, :]

    def send_b(o, _):
        peer = lax.rem(s + o, NS)
        remote(pref.at[peer], pbuf.at[s], b_send.at[o], b_recv.at[s], (peer, e)).start()
        return 0

    lax.fori_loop(1, NS, send_b, 0)
    pbuf[s] = pref[s]
    half = 512
    remote(wbuf.at[y_left], wbuf.at[y_left], w_send.at[0], w_recv.at[0], dev_yl).wait_recv()
    w_f = remote(
        wbuf.at[y_left, 0:half], wbuf.at[y_left, 0:half], w_send.at[2], w_recv.at[2], dev_yr
    )
    w_f.start()
    remote(wbuf.at[y_right], wbuf.at[y_right], w_send.at[1], w_recv.at[1], dev_yr).wait_recv()
    w_b = remote(
        wbuf.at[y_right, half : 2 * half], wbuf.at[y_right, half : 2 * half],
        w_send.at[3], w_recv.at[3], dev_yl,
    )
    w_b.start()

    def wait_b(o, _):
        src = lax.rem(s + o, NS)
        remote(pbuf.at[src], pbuf.at[src], b_send.at[o], b_recv.at[src], (src, e)).wait_recv()
        return 0

    lax.fori_loop(1, NS, wait_b, 0)
    for d in range(NS):
        piece = pbuf[d].astype(f32)
        for r in range(4):
            inc[pl.ds(4 * d + r, HEADS, stride=HD), :] = piece[8 * r : 8 * r + 8]
    for h in range(HEADS):
        cols = slice(h * HD, (h + 1) * HD)
        out = loc[:, cols] + jnp.dot(
            qd[:, cols], inc[cols, :].astype(bf16), preferred_element_type=f32
        )
        mean = jnp.mean(out * out, axis=1, keepdims=True)
        gate = 1.0 / (1.0 + jnp.exp(-g_ref[:, cols].astype(f32)))
        act[z, :, cols] = (out * lax.rsqrt(mean + epsilon) * gain_ref[0:1, cols] * gate).astype(
            bf16
        )

    z_right, z_left = lax.rem(z + 1, NZ), lax.rem(z + NZ - 1, NZ)
    dev_zr, dev_zl = (z_right * NY + y, e), (z_left * NY + y, e)

    def at(k):
        return lax.rem(z + k + NZ, NZ)

    def ring(k):
        own_r, own_l = at(1 - k), at(k - 1)
        if k < 4:
            src_r, src_l = act.at[own_r], act.at[own_l]
        else:
            src_r, src_l = act.at[own_r, 0:64], act.at[own_l, 64:128]
        right = remote(src_r, src_r, r_send.at[2 * k - 2], r_recv.at[2 * k - 2], dev_zr)
        left = remote(src_l, src_l, r_send.at[2 * k - 1], r_recv.at[2 * k - 1], dev_zl)
        right.start()
        left.start()
        return right, left

    def ring_wait(k):
        got_r, got_l = at(-k), at(k)
        if k < 4:
            dst_r, dst_l = act.at[got_r], act.at[got_l]
        else:
            dst_r, dst_l = act.at[got_r, 0:64], act.at[got_l, 64:128]
        remote(dst_r, dst_r, r_send.at[2 * k - 2], r_recv.at[2 * k - 2], dev_zl).wait_recv()
        remote(dst_l, dst_l, r_send.at[2 * k - 1], r_recv.at[2 * k - 1], dev_zr).wait_recv()

    sibling = (s, e + 1 - 2 * c)
    mine = pl.ds(pl.multiple_of(c * 64, 64), 64)
    other = pl.ds(pl.multiple_of((1 - c) * 64, 64), 64)

    def product(k):
        blk = at(k)
        pb[blk] = jnp.dot(act[blk], wcat[...], preferred_element_type=f32).astype(bf16)
        remote(
            pb.at[blk, other], sb.at[blk], sb_send.at[blk], sb_recv.at[blk], sibling
        ).start()

    def pass_on(k):
        blk = at(k)
        remote(
            pb.at[blk, other], sb.at[blk], sb_send.at[blk], sb_recv.at[blk], sibling
        ).wait_recv()
        both = (pb[blk, mine].astype(f32) + sb[blk].astype(f32)).astype(bf16)
        qb[blk] = both

        @pl.when(blk != e)
        def _():
            remote(qb.at[blk], rs.at[e], rs_send.at[blk], rs_recv.at[e], (s, blk)).start()

        @pl.when(blk == e)
        def _():
            rs[e] = both

    sends = [ring(1)]
    wl.wait()
    remote(
        wbuf.at[y_far, 0:half], wbuf.at[y_far, 0:half], w_send.at[2], w_recv.at[2], dev_yl
    ).wait_recv()
    remote(
        wbuf.at[y_far, half : 2 * half], wbuf.at[y_far, half : 2 * half],
        w_send.at[3], w_recv.at[3], dev_yr,
    ).wait_recv()
    for part in range(8):
        rows = slice(part * 128, part * 128 + 128)
        acc = jnp.zeros((128, NY * COLS), f32)
        for i in range(NY):
            place = (iota((COLS, NY * COLS), 1) == iota((COLS, NY * COLS), 0) + i * COLS)
            acc += jnp.dot(
                wbuf[i, rows, :], place.astype(f32).astype(bf16), preferred_element_type=f32
            )
        wcat[rows, :] = acc.astype(bf16)
    product(0)
    ring_wait(1)
    sends.append(ring(2))
    product(-1)
    product(1)
    pass_on(0)
    ring_wait(2)
    sends.append(ring(3))
    product(-2)
    product(2)
    pass_on(-1)
    pass_on(1)
    ring_wait(3)
    sends.append(ring(4))
    product(-3)
    product(3)
    pass_on(-2)
    pass_on(2)
    ring_wait(4)
    product(4)
    pass_on(-3)
    pass_on(3)
    pass_on(4)

    def wait_rs(o, _):
        src = lax.rem(e + o, NE)
        remote(rs.at[src], rs.at[src], rs_send.at[src], rs_recv.at[src], (s, src)).wait_recv()
        return 0

    lax.fori_loop(1, NE, wait_rs, 0)
    halves = []
    for core in range(2):
        acc = rs[core].astype(f32)
        for x in range(1, 4):
            acc += rs[2 * x + core].astype(f32)
        halves.append(acc.astype(bf16))
    block = jnp.concatenate(halves, axis=0)
    for i in range(NY):
        take = (iota((NY * COLS, COLS), 0) == iota((NY * COLS, COLS), 1) + i * COLS)
        ysend[i] = jnp.dot(
            block, take.astype(f32).astype(bf16), preferred_element_type=f32
        ).astype(bf16)

    def send_y(o):
        peer = lax.rem(y + o, NY)
        return remote(
            ysend.at[peer], yrecv.at[y], y_send.at[o], y_recv.at[y], (z * NY + peer, e)
        )

    for o in range(1, NY):
        send_y(o).start()
    yrecv[y] = ysend[y]
    for o in range(1, NY):
        src = lax.rem(y + o, NY)
        remote(
            yrecv.at[src], yrecv.at[src], y_send.at[o], y_recv.at[src], (z * NY + src, e)
        ).wait_recv()
    for i in range(NY):
        rows = slice(i * TOK, (i + 1) * TOK)
        after_ref[rows, :] = res_ref[rows, :].astype(f32) + yrecv[i].astype(f32)

    def drain_state(o, _):
        peer = lax.rem(s + o, NS)
        remote(ub.at[peer], rbuf.at[s], a_send.at[o], a_recv.at[s], (peer, e)).wait_send()
        remote(pref.at[peer], pbuf.at[s], b_send.at[o], b_recv.at[s], (peer, e)).wait_send()
        return 0

    lax.fori_loop(1, NS, drain_state, 0)
    for copy in (w_r, w_l, w_f, w_b):
        copy.wait_send()
    for right, left in sends:
        right.wait_send()
        left.wait_send()
    for blk in range(NZ):
        remote(
            pb.at[blk, other], sb.at[blk], sb_send.at[blk], sb_recv.at[blk], sibling
        ).wait_send()

        @pl.when(blk != e)
        def _():
            remote(qb.at[blk], rs.at[e], rs_send.at[blk], rs_recv.at[e], (s, blk)).wait_send()

    for o in range(1, NY):
        send_y(o).wait_send()


def attention(query, key_in, value_in, gate_in, log_decay, state_in, attn_gain, w_out, residual):
    vmem = pl.BlockSpec(memory_space=pltpu.VMEM)
    dma = pltpu.SemaphoreType.DMA
    wide = HEADS * HD
    return pl.pallas_call(
        attention_kernel,
        out_shape=(
            jax.ShapeDtypeStruct((NY * TOK, COLS), f32),
            jax.ShapeDtypeStruct((HEADS, 4, HD), f32),
        ),
        in_specs=[vmem] * 7 + [pl.BlockSpec(memory_space=pl.ANY), vmem],
        out_specs=(vmem, vmem),
        scratch_shapes=[
            pltpu.VMEM((TOK, HD), f32),
            pltpu.VMEM((TOK, HD), f32),
            pltpu.VMEM((HD, TOK), f32),
            pltpu.VMEM((TOK, wide), bf16),
            pltpu.VMEM((wide, HD), f32),
            pltpu.VMEM((NS, 48, HD), bf16),
            pltpu.VMEM((NS, 48, HD), bf16),
            pltpu.VMEM((NS, 32, HD), bf16),
            pltpu.VMEM((NS, 32, HD), bf16),
            pltpu.VMEM((wide, HD), f32),
            pltpu.VMEM((TOK, wide), f32),
            pltpu.VMEM((TOK, wide), bf16),
            pltpu.VMEM((NY, wide, COLS), bf16),
            pltpu.VMEM((wide, NY * COLS), bf16),
            pltpu.VMEM((NZ, TOK, wide), bf16),
            pltpu.VMEM((NZ, TOK, NY * COLS), bf16),
            pltpu.VMEM((NZ, 64, NY * COLS), bf16),
            pltpu.VMEM((NZ, 64, NY * COLS), bf16),
            pltpu.VMEM((NE, 64, NY * COLS), bf16),
            pltpu.VMEM((NY, TOK, COLS), bf16),
            pltpu.VMEM((NY, TOK, COLS), bf16),
            dma(()), dma((4,)), dma((4,)), dma((NS,)), dma((NS,)), dma((NS,)), dma((NS,)),
            dma((8,)), dma((8,)), dma((8,)), dma((8,)), dma((8,)), dma((8,)), dma((4,)), dma((4,)),
        ],
        compiler_params=pltpu.CompilerParams(
            collective_id=0, has_side_effects=True, vmem_limit_bytes=48 * 1024 * 1024
        ),
        name="attention",
    )(
        query, key_in, value_in, gate_in, log_decay, state_in.reshape(wide, HD),
        attn_gain.reshape(1, wide), w_out, residual,
    )


def entering_2(part, axis, combine, identity):
    place = lax.axis_index(axis)
    gathered = lax.all_gather(part, axis)
    state = jnp.zeros_like(part) + jnp.asarray(identity, part.dtype)

    def one(lap, state):
        return combine(state, lax.dynamic_index_in_dim(gathered, lap, 0, False))

    return lax.fori_loop(0, place, one, state)


def add_counts(earlier, later_counts):
    return earlier + later_counts


def local(
    residual,
    query,
    key_in,
    value_in,
    gate_in,
    log_decay,
    state_in,
    attn_gain,
    w_out,
    moe_gain,
    router,
    w_gate,
    w_up,
    w_down,
    expert_ids,
    keep_counts,
):
    after_attn, final_rows = attention(
        query, key_in, value_in, gate_in, log_decay, state_in, attn_gain, w_out, residual
    )
    block_rows = residual.shape[0]
    experts_all = router.shape[1]
    logit_part = jnp.dot(after_attn * moe_gain, router, precision=highest)
    choose = (
        expert_ids[:, :, None] == jnp.arange(experts_all, dtype=jnp.int32)[None, None, :]
    ).astype(jnp.float32)
    chosen_part = jnp.einsum("tke,te->tk", choose, logit_part, precision=highest)
    squares, chosen = lax.psum((jnp.sum(after_attn * after_attn, axis=1), chosen_part), "seq")
    inv_rms = lax.rsqrt(squares / D + epsilon)
    chosen = chosen * inv_rms[:, None]
    gate_probs = jnp.stack(
        [jax.nn.sigmoid(chosen[:, 0] - chosen[:, 1]), jax.nn.sigmoid(chosen[:, 1] - chosen[:, 0])],
        axis=1,
    )
    routed_in = (after_attn * inv_rms[:, None] * moe_gain).astype(jnp.bfloat16)
    lanes = lax.axis_size("exp")
    window = w_gate.shape[0] * lanes
    capacity = 5 * block_rows * lanes // (2 * lanes * experts_all)
    top_count = expert_ids.shape[1]
    flat_ids = expert_ids.reshape(block_rows * top_count)
    onehot = (flat_ids[:, None] == jnp.arange(window, dtype=jnp.int32)[None, :]).astype(jnp.int32)
    local_rank = jnp.sum((jnp.cumsum(onehot, axis=0) - onehot) * onehot, axis=1)
    before = entering_2(jnp.sum(onehot, axis=0), "exp", add_counts, jnp.zeros((window,), jnp.int32))
    global_rank = local_rank + jnp.sum(before[None, :] * onehot, axis=1)
    limits = jnp.sum(keep_counts[None, :window] * onehot, axis=1)
    is_kept = (flat_ids < window) & (global_rank < limits)
    slot_hot = ((local_rank[:, None] == jnp.arange(capacity)[None, :]) & is_kept[:, None]).astype(
        jnp.int32
    )
    assign_int = onehot[:, :, None] * slot_hot[:, None, :]
    assign_table = assign_int.astype(jnp.bfloat16)
    token_table = jnp.sum(
        assign_int.reshape(block_rows, top_count, window, capacity), axis=1
    ).astype(jnp.bfloat16)
    sending = jnp.einsum(
        "tec,td->ecd", token_table, routed_in, preferred_element_type=jnp.float32
    ).astype(jnp.bfloat16)
    arrived = lax.all_to_all(sending, "exp", split_axis=0, concat_axis=1, tiled=True)
    contract_dims = (((1,), (1,)), ((), ()))
    portion = lax.all_gather(arrived, "seq", axis=2, tiled=True)
    gate_cols = w_gate[0]
    up_cols = w_up[0]
    gate_add = lax.dot_general(
        portion[0], gate_cols, contract_dims, preferred_element_type=jnp.float32
    )
    up_add = lax.dot_general(portion[0], up_cols, contract_dims, preferred_element_type=jnp.float32)
    hidden = (jax.nn.silu(gate_add) * up_add).astype(jnp.bfloat16)
    down_rows = w_down[0]
    result = jnp.dot(
        lax.all_gather(hidden, "seq", axis=1, tiled=True),
        down_rows,
        preferred_element_type=jnp.float32,
    )
    expert_out = result.astype(jnp.bfloat16)[None]
    returned = lax.all_to_all(expert_out, "exp", split_axis=1, concat_axis=0, tiled=True)
    picked = jnp.einsum(
        "aec,ecd->ad", assign_table, returned, preferred_element_type=jnp.float32
    ).reshape(block_rows, top_count, -1)
    weight = jnp.where(is_kept.reshape(block_rows, top_count), gate_probs, 0.0)
    expert_sum = jnp.sum(picked * weight[:, :, None], axis=1)
    return ((after_attn + expert_sum).astype(jnp.bfloat16), final_rows)


def solution(mesh):
    in_specs = (
        P("exp", "seq"),
        P("seq", "exp"),
        P("seq", "exp"),
        P("seq", "exp"),
        P("seq", "exp"),
        P("seq", "exp"),
        P("exp", None, None),
        P("exp"),
        P("exp", "seq"),
        P("seq"),
        P("seq", None),
        P("exp", "seq", None),
        P("exp", "seq", None),
        P("exp", None, "seq"),
        P("exp", None),
        P(),
    )
    out_specs = (P("exp", "seq"), P("exp", "seq", None))
    return jax.shard_map(local, mesh=mesh, in_specs=in_specs, out_specs=out_specs, check_vma=False)
```

```python
import jax
import jax.numpy as jnp
from jax import lax
from jax.experimental import pallas as pl
from jax.experimental.pallas import tpu as pltpu
from jax.sharding import PartitionSpec as P

f32, bf16 = jnp.float32, jnp.bfloat16
highest = lax.Precision.HIGHEST
epsilon = 1e-05
D = 6144
NS, NE, NY, NZ = 32, 8, 4, 8
HEADS, HD, TOK = 8, 128, 128
COLS = 192
MESH = pl.DeviceIdType.MESH


def silu(v):
    return v / (1.0 + jnp.exp(-v))


def iota(shape, dim):
    return lax.broadcasted_iota(jnp.int32, shape, dim)


def remote(src, dst, send, recv, dev):
    return pltpu.make_async_remote_copy(
        src_ref=src, dst_ref=dst, send_sem=send, recv_sem=recv, device_id=dev, device_id_type=MESH
    )


def enter(s, e):
    barrier = pltpu.get_barrier_semaphore()

    def seq_signal(o, _):
        pl.semaphore_signal(
            barrier, inc=1, device_id=(lax.rem(s + o, NS), e), device_id_type=MESH
        )
        return 0

    def exp_signal(o, _):
        pl.semaphore_signal(
            barrier, inc=1, device_id=(s, lax.rem(e + o, NE)), device_id_type=MESH
        )
        return 0

    lax.fori_loop(1, NS, seq_signal, 0)
    lax.fori_loop(1, NE, exp_signal, 0)
    return barrier


def layer_kernel(
    q_ref, k_ref, v_ref, g_ref, ld_ref, st_ref, gain_ref, w_hbm, res_ref,
    mgain_ref, router_ref, ids_ref, keep_ref, wg_hbm, wu_hbm, wd_hbm,
    out_ref, fin_ref,
    ldp, lcol, lrow, kbf, upd, ub, rbuf, pref, pbuf, inc, loc, qd,
    wcat, act, pb, sb, qb, rs, ysend, yrecv,
    after, slot_mask, combine, place, cnt, stat, inv_send, inv_recv,
    disp, disp_in, back, back_in, x_a, x_b, x_r, h_a, h_b, h_r, wg, wu, wd, acc_g, acc_u,
    w_local, w_send, w_recv, a_send, a_recv, b_send, b_recv,
    r_send, r_recv, sb_send, sb_recv, rs_send, rs_recv, y_send, y_recv,
    big, c_send, c_recv, t_send, t_recv, i_send, i_recv, d_send, d_recv, o_send, o_recv,
    ag_send, ag_recv,
):
    s = lax.axis_index("seq")
    e = lax.axis_index("exp")
    y, z = lax.rem(s, NY), s // NY
    c = lax.rem(e, 2)
    barrier = enter(s, e)

    def cols_of(at, first, count):
        return pl.ds(pl.multiple_of(at * COLS + first, 16), count)

    wl = pltpu.make_async_copy(w_hbm, wcat.at[cols_of(y, 0, COLS)], w_local)
    wl.start()
    loads = [
        pltpu.make_async_copy(src, dst, big.at[i])
        for i, (src, dst) in enumerate(((wg_hbm, wg), (wu_hbm, wu), (wd_hbm, wd)))
    ]
    for load in loads:
        load.start()

    ids = [ids_ref[k : k + 1, :] for k in range(2)]
    hot = [(iota((8, 512), 0) == ids[k]).astype(f32) for k in range(2)]
    held = hot[0] + hot[1]

    def exp_copy(src, dst, send, recv, o):
        peer = lax.rem(e + o, NE)
        return remote(src(peer), dst.at[e], send.at[o], recv.at[e], (s, peer))

    def exp_wait(dst, send, recv):
        def one(o, _):
            src = lax.rem(e + o, NE)
            remote(dst.at[src], dst.at[src], send.at[o], recv.at[src], (s, src)).wait_recv()
            return 0

        lax.fori_loop(1, NE, one, 0)

    def exp_start(src, dst, send, recv):
        def one(o, _):
            exp_copy(src, dst, send, recv, o).start()
            return 0

        lax.fori_loop(1, NE, one, 0)

    def count_tokens():
        totals = jnp.sum(held, axis=1, keepdims=True)
        cnt[e] = jnp.broadcast_to(totals, (8, 128))
        exp_start(lambda peer: cnt.at[e], cnt, c_send, c_recv)

    def ranks():
        later = (iota((512, 512), 0) < iota((512, 512), 1)).astype(f32).astype(bf16)
        return jnp.dot(held.astype(bf16), later, preferred_element_type=f32)

    def slots(earlier):
        found = []
        for k in range(2):
            rank = jnp.sum(hot[k] * earlier, axis=0, keepdims=True).astype(jnp.int32)
            found.append(jnp.where(ids[k] < 8, ids[k] * 128 + rank, -1))
        return found

    def prepare():
        for g in range(3):
            for b in range(NE):
                lane = iota((128, 384), 0) - 40 * g
                hit = (iota((128, 384), 1) == lane + 40 * b) & (lane >= 0) & (lane < 40)
                place[g, b * 128 : b * 128 + 128, :] = jnp.where(hit, 1.0, 0.0).astype(bf16)
        slot = slots(ranks())
        for b in range(NE):
            at_row = iota((128, 512), 0) + b * 128
            hit = (at_row == slot[0]) | (at_row == slot[1])
            slot_mask[b * 128 : b * 128 + 128, :] = jnp.where(hit, 1.0, 0.0).astype(bf16)

    def by_lanes(a, b):
        return lax.dot_general(a, b, (((1,), (1,)), ((), ())), preferred_element_type=f32)

    def split(row):
        one = row.astype(bf16).astype(f32)
        two = (row - one).astype(bf16).astype(f32)
        return jnp.concatenate([one, two, row - one - two] + [jnp.zeros_like(row)] * 5, axis=0)

    def gather(a, b, turn, cut, hook):
        z_r, z_l = lax.rem(z + 1, NZ) * NY + y, lax.rem(z + NZ - 1, NZ) * NY + y
        y_r, y_l = z * NY + lax.rem(y + 1, NY), z * NY + lax.rem(y + NY - 1, NY)
        dev_z, dev_y = ((z_r, e), (z_l, e)), ((y_r, e), (y_l, e))
        rows_a, rows_b = a.shape[2], b.shape[2]
        started = []

        def zz(k):
            return lax.rem(z + k + NZ, NZ)

        def yy(k):
            return lax.rem(y + k + NY, NY)

        def move(ref, index, dev):
            return remote(ref, ref, ag_send.at[turn, index], ag_recv.at[turn, index], dev)

        def go(ref, index, dev):
            started.append(move(ref, index, dev))
            started[-1].start()

        def come(ref, index, dev):
            move(ref, index, dev).wait_recv()

        def a_y(step, way):
            k = (1 - step if way == 0 else step - 1) if step > 0 else 0
            return k

        def a1(step, do, take):
            for way in range(2):
                sign = -1 if way == 0 else 1
                k = sign * (step if take else step - 1)
                ref = a.at[z, yy(k)]
                if step == 2:
                    ref = a.at[z, yy(k), way * (rows_a // 2) : (way + 1) * (rows_a // 2)]
                do(ref, 2 * step - 2 + way, dev_y[1 - way if take else way])

        def a2(step, do, take):
            for way in range(2):
                sign = -1 if way == 0 else 1
                k = sign * (step if take else step - 1)
                ref = a.at[zz(k)]
                if step == 4:
                    ref = a.at[zz(k), 2 * way : 2 * way + 2]
                do(ref, 4 + 2 * step - 2 + way, dev_z[1 - way if take else way])

        def b1(step, do, take):
            for way in range(2):
                sign = -1 if way == 0 else 1
                k = sign * (step if take else step - 1)
                ref = b.at[zz(k), y]
                if step == 4:
                    ref = b.at[zz(k), y, 0:cut] if way == 0 else b.at[zz(k), y, cut:rows_b]
                do(ref, 12 + 2 * step - 2 + way, dev_z[1 - way if take else way])

        def b2(step, at_z, do, take):
            for way in range(2):
                sign = -1 if way == 0 else 1
                k = sign * (step if take else step - 1)
                ref = b.at[zz(at_z), yy(k)]
                if step == 2:
                    ref = (
                        b.at[zz(at_z), yy(k), 0:cut]
                        if way == 0
                        else b.at[zz(at_z), yy(k), cut:rows_b]
                    )
                index = 20 + 4 * (at_z + 3) + 2 * step - 2 + way
                do(ref, index, dev_y[1 - way if take else way])

        def turn_b(*ks):
            for k in ks:
                b2(1, k, come, True)
                b2(2, k, go, False)

        a1(1, go, False)
        b1(1, go, False)
        b2(1, 0, go, False)
        a1(1, come, True)
        a1(2, go, False)
        hook()
        b1(1, come, True)
        b1(2, go, False)
        b2(1, -1, go, False)
        b2(1, 1, go, False)
        a1(2, come, True)
        a2(1, go, False)
        turn_b(0)
        b1(2, come, True)
        b1(3, go, False)
        b2(1, -2, go, False)
        b2(1, 2, go, False)
        turn_b(-1, 1)
        b1(3, come, True)
        b1(4, go, False)
        b2(1, -3, go, False)
        b2(1, 3, go, False)
        a2(1, come, True)
        a2(2, go, False)
        b1(4, come, True)
        b2(1, 4, go, False)
        turn_b(-2, 2)
        a2(2, come, True)
        a2(3, go, False)
        turn_b(-3, 3)
        a2(3, come, True)
        a2(4, go, False)
        turn_b(4)
        a2(4, come, True)
        for k in range(-3, 5):
            b2(2, k, come, True)
        return started

    def unpack(src, first, rows, dst):
        swap = (iota((128, 128), 0) == lax.rem(iota((128, 128), 1) + 64, 128)).astype(f32)
        swap = swap.astype(bf16)

        def one(i, _):
            zi, yi = i // NY, lax.rem(i, NY)
            part = src[zi, yi, first : first + rows, :]
            dst[zi, yi, 0:rows, :] = part
            dst[zi, yi, rows : 2 * rows, :] = jnp.dot(
                part, swap, preferred_element_type=f32
            ).astype(bf16)
            return 0

        lax.fori_loop(0, NS, one, 0)

    def own_pieces(full, a, b):
        rows = a.shape[2]
        a[z, y] = full[:, 0:128].astype(bf16)
        b[z, y, 0:rows, :] = full[:, 128:256].astype(bf16)
        rest = jnp.where(iota((rows, 128), 1) < 64, full[:, 256:384], 0.0)
        packed = rest[0 : rows // 2] + pltpu.roll(rest[rows // 2 : rows], 64, 1)
        b[z, y, rows : rows + rows // 2, :] = packed.astype(bf16)

    drains = []

    def experts():
        eye = iota((COLS, COLS), 0) == iota((COLS, COLS), 1)
        gain_col = jnp.sum(jnp.where(eye, mgain_ref[...], 0.0), axis=1, keepdims=True)
        rows = after[...]
        squares = jnp.sum(rows * rows, axis=0, keepdims=True)
        logits = jnp.dot(
            router_ref[...] * mgain_ref[...], rows, preferred_element_type=f32, precision=highest
        )
        lane_e = iota((32, 512), 0)
        signed = (lane_e == ids[0]).astype(f32) - (lane_e == ids[1]).astype(f32)
        diff = jnp.sum(signed * logits, axis=0, keepdims=True)
        parts = [r[:, i * 128 : i * 128 + 128] for r in (squares, diff) for i in range(4)]
        stat[s] = jnp.concatenate(parts, axis=0)

        def send_t(o, _):
            peer = lax.rem(s + o, NS)
            remote(stat.at[s], stat.at[s], t_send.at[o], t_recv.at[s], (peer, e)).start()
            return 0

        scaled = (rows * gain_col).astype(bf16)
        packed = [jnp.zeros((64, 128), f32) for _ in range(NE)]
        for g in range(3):
            chosen = by_lanes(scaled[64 * g : 64 * g + 64, :], slot_mask[...])
            for b in range(NE):
                tile = chosen[:, b * 128 : b * 128 + 128]
                packed[b] = packed[b] + (pltpu.roll(tile, 40 * g, 1) if g else tile)
        for b in range(NE):
            disp[b] = packed[b].astype(bf16)
        exp_start(lambda peer: disp.at[peer], disp_in, d_send, d_recv)
        lax.fori_loop(1, NS, send_t, 0)
        disp_in[e] = disp[e]
        exp_wait(disp_in, d_send, d_recv)
        arrived = jnp.concatenate([disp_in[b] for b in range(NE)], axis=1)
        full = jnp.concatenate(
            [jnp.dot(arrived, place[g], preferred_element_type=f32) for g in range(3)], axis=0
        )
        own_pieces(full, x_a, x_b)

        def weights():
            def wait_t(o, _):
                src = lax.rem(s + o, NS)
                remote(
                    stat.at[src], stat.at[src], t_send.at[o], t_recv.at[src], (src, e)
                ).wait_recv()
                return 0

            lax.fori_loop(1, NS, wait_t, 0)
            total = lax.fori_loop(0, NS, lambda j, t: t + stat[j], jnp.zeros((8, 128), f32))
            sq = jnp.concatenate([total[i : i + 1] for i in range(4)], axis=1)
            gap = jnp.concatenate([total[i : i + 1] for i in range(4, 8)], axis=1)
            inv = lax.rsqrt(sq / D + epsilon)
            gap = gap * inv
            per_slot = by_lanes(split(inv).astype(bf16), slot_mask[...])
            per_slot = per_slot[0:1] + per_slot[1:2] + per_slot[2:3]
            for b in range(NE):
                inv_send[b] = jnp.broadcast_to(per_slot[:, b * 128 : b * 128 + 128], (8, 128))
            exp_start(lambda peer: inv_send.at[peer], inv_recv, i_send, i_recv)
            inv_recv[e] = inv_send[e]
            exp_wait(cnt, c_send, c_recv)
            before = lax.fori_loop(
                0, NE, lambda j, t: t + jnp.where(j < e, cnt[j], 0.0), jnp.zeros((8, 128), f32)
            )
            keep = jnp.where(iota((8, 32), 0) == iota((8, 32), 1), keep_ref[...], 0).astype(f32)
            limit = jnp.sum(keep, axis=1, keepdims=True) - before[:, 0:1]
            earlier = ranks()
            fits = (earlier < limit).astype(f32)
            slot = slots(earlier)
            prob = [1.0 / (1.0 + jnp.exp(-gap)), 1.0 / (1.0 + jnp.exp(gap))]
            weight = [jnp.sum(hot[k] * fits, axis=0, keepdims=True) * prob[k] for k in range(2)]
            for b in range(NE):
                at_row = iota((128, 512), 0) + b * 128
                value = jnp.where(at_row == slot[0], weight[0], 0.0)
                value = jnp.where(at_row == slot[1], weight[1], value)
                combine[b * 128 : b * 128 + 128, :] = value.astype(bf16)

        drains.extend(gather(x_a, x_b, 0, 144, weights))
        unpack(x_b, 192, 96, x_r)
        exp_wait(inv_recv, i_send, i_recv)
        row = jnp.concatenate([inv_recv[b][0:1] for b in range(NE)], axis=1)
        inv_row = jnp.dot(split(row).astype(bf16), place[0], preferred_element_type=f32)
        inv_row = inv_row[0:1] + inv_row[1:2] + inv_row[2:3]
        loads[0].wait()
        loads[1].wait()
        for zi in range(NZ):
            k = slice(zi * 768, zi * 768 + 768)
            piece = jnp.concatenate(
                [
                    x_a[zi].reshape(768, 128),
                    x_b[zi, :, 0:192, :].reshape(768, 128),
                    x_r[zi].reshape(768, 128),
                ],
                axis=1,
            )
            for weight, acc in ((wg, acc_g), (wu, acc_u)):
                part = jnp.dot(weight[:, k], piece, preferred_element_type=f32)
                acc[...] = part if zi == 0 else acc[...] + part
        gate = acc_g[...] * inv_row
        own_pieces(silu(gate) * (acc_u[...] * inv_row), h_a, h_b)
        drains.extend(gather(h_a, h_b, 1, 224, lambda: None))
        unpack(h_b, 288, 144, h_r)
        loads[2].wait()
        total = jnp.zeros((COLS, 384), f32)
        for zi in range(NZ):
            k = slice(zi * 1152, zi * 1152 + 1152)
            piece = jnp.concatenate(
                [
                    h_a[zi].reshape(1152, 128),
                    h_b[zi, :, 0:288, :].reshape(1152, 128),
                    h_r[zi].reshape(1152, 128),
                ],
                axis=1,
            )
            total = total + jnp.dot(wd[:, k], piece, preferred_element_type=f32)
        result = total.astype(bf16)
        packed = by_lanes(result[0:64], place[0])
        for g in range(1, 3):
            packed = packed + by_lanes(result[64 * g : 64 * g + 64], place[g])
        for b in range(NE):
            back[b] = packed[:, b * 128 : b * 128 + 128].astype(bf16)
        exp_start(lambda peer: back.at[peer], back_in, o_send, o_recv)
        back_in[e] = back[e]
        exp_wait(back_in, o_send, o_recv)
        tiles = [back_in[b].astype(f32) for b in range(NE)]
        for g in range(3):
            moved = [pltpu.roll(t, 128 - 40 * g, 1) if g else t for t in tiles]
            picked = jnp.dot(
                jnp.concatenate(moved, axis=1).astype(bf16), combine[...],
                preferred_element_type=f32,
            )
            r = slice(64 * g, 64 * g + 64)
            out_ref[r, :] = (after[r, :] + picked).astype(bf16)

    def drain_experts():
        for copy in drains:
            copy.wait_send()

        def one(o, _):
            exp_copy(lambda peer: cnt.at[e], cnt, c_send, c_recv, o).wait_send()
            exp_copy(lambda peer: disp.at[peer], disp_in, d_send, d_recv, o).wait_send()
            exp_copy(lambda peer: inv_send.at[peer], inv_recv, i_send, i_recv, o).wait_send()
            exp_copy(lambda peer: back.at[peer], back_in, o_send, o_recv, o).wait_send()
            return 0

        def stats(o, _):
            peer = lax.rem(s + o, NS)
            remote(stat.at[s], stat.at[s], t_send.at[o], t_recv.at[s], (peer, e)).wait_send()
            return 0

        lax.fori_loop(1, NE, one, 0)
        lax.fori_loop(1, NS, stats, 0)

    ldp[...] = jnp.zeros_like(ldp)
    ldp[0:HEADS, :] = ld_ref[...]
    tri = (iota((TOK, TOK), 0) <= iota((TOK, TOK), 1)).astype(f32)
    run = jnp.dot(ldp[...], tri, preferred_element_type=f32, precision=highest)
    lrow[...] = run
    lcol[...] = run.T
    for h in range(HEADS):
        cols = slice(h * HD, (h + 1) * HD)
        kh = silu(k_ref[:, cols].astype(f32))
        kbf[:, cols] = kh.astype(bf16)
        tail = jnp.exp(lcol[TOK - 1 : TOK, h : h + 1] - lcol[:, h : h + 1])
        kd = (kh * tail).T.astype(bf16)
        upd[cols, :] = jnp.dot(kd, v_ref[:, cols], preferred_element_type=f32)
    total = jnp.broadcast_to(lrow[0:HEADS, TOK - 1 : TOK], (HEADS, HD))
    high = total.astype(bf16).astype(f32)
    logs = jnp.concatenate([high, total - high], axis=0).astype(bf16)
    for d in range(NS):
        rows = [upd[pl.ds(4 * d + r, HEADS, stride=HD), :] for r in range(4)]
        ub[d, 0:32, :] = jnp.concatenate(rows, axis=0).astype(bf16)
        ub[d, 32:48, :] = logs

    pl.semaphore_wait(barrier, NS - 1 + NE - 1)

    def send_a(o, _):
        peer = lax.rem(s + o, NS)
        remote(ub.at[peer], rbuf.at[s], a_send.at[o], a_recv.at[s], (peer, e)).start()
        return 0

    lax.fori_loop(1, NS, send_a, 0)
    count_tokens()
    rbuf[s] = ub[s]
    y_right, y_left = lax.rem(y + 1, NY), lax.rem(y + NY - 1, NY)
    y_far = lax.rem(y + 2, NY)
    dev_yr, dev_yl = (z * NY + y_right, e), (z * NY + y_left, e)
    w_r = remote(w_hbm, wcat.at[cols_of(y, 0, COLS)], w_send.at[0], w_recv.at[0], dev_yr)
    w_l = remote(w_hbm, wcat.at[cols_of(y, 0, COLS)], w_send.at[1], w_recv.at[1], dev_yl)
    w_r.start()
    w_l.start()

    causal = iota((TOK, TOK), 0) >= iota((TOK, TOK), 1)
    for h in range(HEADS):
        cols = slice(h * HD, (h + 1) * HD)
        qh = silu(q_ref[:, cols].astype(f32))
        lc = lcol[:, h : h + 1]
        gap = lc - lrow[h : h + 1, :]
        decay = jnp.where(causal, jnp.exp(jnp.where(causal, gap, 0.0)), 0.0)
        scores = lax.dot_general(
            qh.astype(bf16), kbf[:, cols], (((1,), (1,)), ((), ())), preferred_element_type=f32
        )
        loc[:, cols] = jnp.dot(
            (scores * decay).astype(bf16), v_ref[:, cols], preferred_element_type=f32
        )
        qd[:, cols] = (qh * jnp.exp(lc)).astype(bf16)

    def wait_a(o, _):
        src = lax.rem(s + o, NS)
        remote(rbuf.at[src], rbuf.at[src], a_send.at[o], a_recv.at[src], (src, e)).wait_recv()
        return 0

    lax.fori_loop(1, NS, wait_a, 0)
    start = jnp.concatenate(
        [st_ref[pl.ds(4 * s + r, HEADS, stride=HD), :] for r in range(4)], axis=0
    )

    def scan(j, state):
        pref[j] = state.astype(bf16)
        piece = rbuf[j].astype(f32)
        dec = jnp.exp(piece[32:40] + piece[40:48])
        return state * jnp.concatenate([dec] * 4, axis=0) + piece[0:32]

    last = lax.fori_loop(0, NS, scan, start)
    for r in range(4):
        for h in range(HEADS):
            fin_ref[h, r : r + 1, :] = last[8 * r + h : 8 * r + h + 1, :]

    def send_b(o, _):
        peer = lax.rem(s + o, NS)
        remote(pref.at[peer], pbuf.at[s], b_send.at[o], b_recv.at[s], (peer, e)).start()
        return 0

    lax.fori_loop(1, NS, send_b, 0)
    pbuf[s] = pref[s]
    half = COLS // 2

    def w_half(at, part):
        return wcat.at[cols_of(at, part * half, half)]

    w_whole = [wcat.at[cols_of(at, 0, COLS)] for at in (y_left, y_right)]
    remote(w_whole[0], w_whole[0], w_send.at[0], w_recv.at[0], dev_yl).wait_recv()
    w_f = remote(w_half(y_left, 0), w_half(y_left, 0), w_send.at[2], w_recv.at[2], dev_yr)
    w_f.start()
    remote(w_whole[1], w_whole[1], w_send.at[1], w_recv.at[1], dev_yr).wait_recv()
    w_b = remote(w_half(y_right, 1), w_half(y_right, 1), w_send.at[3], w_recv.at[3], dev_yl)
    w_b.start()
    prepare()

    def wait_b(o, _):
        src = lax.rem(s + o, NS)
        remote(pbuf.at[src], pbuf.at[src], b_send.at[o], b_recv.at[src], (src, e)).wait_recv()
        return 0

    lax.fori_loop(1, NS, wait_b, 0)
    for d in range(NS):
        piece = pbuf[d].astype(f32)
        for r in range(4):
            inc[pl.ds(4 * d + r, HEADS, stride=HD), :] = piece[8 * r : 8 * r + 8]
    for h in range(HEADS):
        cols = slice(h * HD, (h + 1) * HD)
        out = loc[:, cols] + jnp.dot(
            qd[:, cols], inc[cols, :].astype(bf16), preferred_element_type=f32
        )
        mean = jnp.mean(out * out, axis=1, keepdims=True)
        gate = 1.0 / (1.0 + jnp.exp(-g_ref[:, cols].astype(f32)))
        act[z, :, cols] = (out * lax.rsqrt(mean + epsilon) * gain_ref[0:1, cols] * gate).astype(
            bf16
        )

    z_right, z_left = lax.rem(z + 1, NZ), lax.rem(z + NZ - 1, NZ)
    dev_zr, dev_zl = (z_right * NY + y, e), (z_left * NY + y, e)

    def at(k):
        return lax.rem(z + k + NZ, NZ)

    def ring(k):
        own_r, own_l = at(1 - k), at(k - 1)
        if k < 4:
            src_r, src_l = act.at[own_r], act.at[own_l]
        else:
            src_r, src_l = act.at[own_r, 0:64], act.at[own_l, 64:128]
        right = remote(src_r, src_r, r_send.at[2 * k - 2], r_recv.at[2 * k - 2], dev_zr)
        left = remote(src_l, src_l, r_send.at[2 * k - 1], r_recv.at[2 * k - 1], dev_zl)
        right.start()
        left.start()
        return right, left

    def ring_wait(k):
        got_r, got_l = at(-k), at(k)
        if k < 4:
            dst_r, dst_l = act.at[got_r], act.at[got_l]
        else:
            dst_r, dst_l = act.at[got_r, 0:64], act.at[got_l, 64:128]
        remote(dst_r, dst_r, r_send.at[2 * k - 2], r_recv.at[2 * k - 2], dev_zl).wait_recv()
        remote(dst_l, dst_l, r_send.at[2 * k - 1], r_recv.at[2 * k - 1], dev_zr).wait_recv()

    sibling = (s, e + 1 - 2 * c)
    mine = pl.ds(pl.multiple_of(c * 384, 384), 384)
    other = pl.ds(pl.multiple_of((1 - c) * 384, 384), 384)

    def product(k):
        blk = at(k)
        pb[blk] = lax.dot_general(
            wcat[...], act[blk], (((1,), (1,)), ((), ())), preferred_element_type=f32
        ).astype(bf16)
        remote(
            pb.at[blk, other], sb.at[blk], sb_send.at[blk], sb_recv.at[blk], sibling
        ).start()

    def pass_on(k):
        blk = at(k)
        remote(
            pb.at[blk, other], sb.at[blk], sb_send.at[blk], sb_recv.at[blk], sibling
        ).wait_recv()
        both = (pb[blk, mine].astype(f32) + sb[blk].astype(f32)).astype(bf16)
        qb[blk] = both

        @pl.when(blk != e)
        def _():
            remote(qb.at[blk], rs.at[e], rs_send.at[blk], rs_recv.at[e], (s, blk)).start()

        @pl.when(blk == e)
        def _():
            rs[e] = both

    sends = [ring(1)]
    wl.wait()
    remote(
        w_half(y_far, 0), w_half(y_far, 0), w_send.at[2], w_recv.at[2], dev_yl
    ).wait_recv()
    remote(
        w_half(y_far, 1), w_half(y_far, 1), w_send.at[3], w_recv.at[3], dev_yr
    ).wait_recv()
    product(0)
    ring_wait(1)
    sends.append(ring(2))
    product(-1)
    product(1)
    pass_on(0)
    ring_wait(2)
    sends.append(ring(3))
    product(-2)
    product(2)
    pass_on(-1)
    pass_on(1)
    ring_wait(3)
    sends.append(ring(4))
    product(-3)
    product(3)
    pass_on(-2)
    pass_on(2)
    ring_wait(4)
    product(4)
    pass_on(-3)
    pass_on(3)
    pass_on(4)

    def wait_rs(o, _):
        src = lax.rem(e + o, NE)
        remote(rs.at[src], rs.at[src], rs_send.at[src], rs_recv.at[src], (s, src)).wait_recv()
        return 0

    lax.fori_loop(1, NE, wait_rs, 0)
    for core in range(2):
        acc = rs[core].astype(f32)
        for x in range(1, 4):
            acc += rs[2 * x + core].astype(f32)
        ysend[core * 384 : core * 384 + 384, :] = acc.astype(bf16)

    def send_y(o):
        peer = lax.rem(y + o, NY)
        return remote(
            ysend.at[cols_of(peer, 0, COLS)], yrecv.at[y], y_send.at[o], y_recv.at[y],
            (z * NY + peer, e),
        )

    for o in range(1, NY):
        send_y(o).start()
    yrecv[y] = ysend[cols_of(y, 0, COLS), :]
    for o in range(1, NY):
        src = lax.rem(y + o, NY)
        remote(
            yrecv.at[src], yrecv.at[src], y_send.at[o], y_recv.at[src], (z * NY + src, e)
        ).wait_recv()
    for i in range(NY):
        cols = slice(i * TOK, (i + 1) * TOK)
        after[:, cols] = res_ref[:, cols].astype(f32) + yrecv[i].astype(f32)

    experts()

    def drain_state(o, _):
        peer = lax.rem(s + o, NS)
        remote(ub.at[peer], rbuf.at[s], a_send.at[o], a_recv.at[s], (peer, e)).wait_send()
        remote(pref.at[peer], pbuf.at[s], b_send.at[o], b_recv.at[s], (peer, e)).wait_send()
        return 0

    lax.fori_loop(1, NS, drain_state, 0)
    for copy in (w_r, w_l, w_f, w_b):
        copy.wait_send()
    for right, left in sends:
        right.wait_send()
        left.wait_send()
    for blk in range(NZ):
        remote(
            pb.at[blk, other], sb.at[blk], sb_send.at[blk], sb_recv.at[blk], sibling
        ).wait_send()

        @pl.when(blk != e)
        def _():
            remote(qb.at[blk], rs.at[e], rs_send.at[blk], rs_recv.at[e], (s, blk)).wait_send()

    for o in range(1, NY):
        send_y(o).wait_send()
    drain_experts()


def local(
    residual, query, key_in, value_in, gate_in, log_decay, state_in, attn_gain, w_out,
    moe_gain, router, w_gate, w_up, w_down, expert_ids, keep_counts,
):
    vmem = pl.BlockSpec(memory_space=pltpu.VMEM)
    hbm = pl.BlockSpec(memory_space=pl.ANY)
    dma = pltpu.SemaphoreType.DMA
    wide = HEADS * HD
    V = pltpu.VMEM
    out, final = pl.pallas_call(
        layer_kernel,
        out_shape=(
            jax.ShapeDtypeStruct((COLS, NY * TOK), bf16),
            jax.ShapeDtypeStruct((HEADS, 4, HD), f32),
        ),
        in_specs=[vmem] * 7 + [hbm] + [vmem] * 5 + [hbm] * 3,
        out_specs=(vmem, vmem),
        scratch_shapes=[
            V((TOK, HD), f32), V((TOK, HD), f32), V((HD, TOK), f32), V((TOK, wide), bf16),
            V((wide, HD), f32), V((NS, 48, HD), bf16), V((NS, 48, HD), bf16),
            V((NS, 32, HD), bf16), V((NS, 32, HD), bf16), V((wide, HD), f32),
            V((TOK, wide), f32), V((TOK, wide), bf16),
            V((NY * COLS, wide), bf16), V((NZ, TOK, wide), bf16),
            V((NZ, NY * COLS, TOK), bf16), V((NZ, 384, TOK), bf16), V((NZ, 384, TOK), bf16),
            V((NE, 384, TOK), bf16), V((NY * COLS, TOK), bf16), V((NY, COLS, TOK), bf16),
            V((COLS, NY * TOK), f32), V((1024, 512), bf16), V((1024, 512), bf16),
            V((3, 1024, 384), bf16), V((NE, 8, 128), f32), V((NS, 8, 128), f32),
            V((NE, 8, 128), f32), V((NE, 8, 128), f32),
            V((NE, 64, 128), bf16), V((NE, 64, 128), bf16),
            V((NE, 64, 128), bf16), V((NE, 64, 128), bf16),
            V((NZ, NY, 192, 128), bf16), V((NZ, NY, 288, 128), bf16), V((NZ, NY, 192, 128), bf16),
            V((NZ, NY, 288, 128), bf16), V((NZ, NY, 432, 128), bf16), V((NZ, NY, 288, 128), bf16),
            V((288, D), bf16), V((288, D), bf16), V((COLS, 9216), bf16),
            V((288, 384), f32), V((288, 384), f32),
            dma(()), dma((4,)), dma((4,)), dma((NS,)), dma((NS,)), dma((NS,)), dma((NS,)),
            dma((8,)), dma((8,)), dma((8,)), dma((8,)), dma((8,)), dma((8,)), dma((4,)), dma((4,)),
            dma((3,)), dma((8,)), dma((8,)), dma((NS,)), dma((NS,)), dma((8,)), dma((8,)),
            dma((8,)), dma((8,)), dma((8,)), dma((8,)), dma((2, 52)), dma((2, 52)),
        ],
        compiler_params=pltpu.CompilerParams(
            collective_id=0, has_side_effects=True, vmem_limit_bytes=62 * 1024 * 1024
        ),
        name="layer",
    )(
        query, key_in, value_in, gate_in, log_decay.T, state_in.reshape(wide, HD),
        attn_gain.reshape(1, wide), w_out.T, residual.T, moe_gain.reshape(1, COLS), router.T,
        expert_ids.T, keep_counts.reshape(1, 32), w_gate[0], w_up[0], w_down[0].T,
    )
    return out.T, final


def solution(mesh):
    in_specs = (
        P("exp", "seq"),
        P("seq", "exp"),
        P("seq", "exp"),
        P("seq", "exp"),
        P("seq", "exp"),
        P("seq", "exp"),
        P("exp", None, None),
        P("exp"),
        P("exp", "seq"),
        P("seq"),
        P("seq", None),
        P("exp", "seq", None),
        P("exp", "seq", None),
        P("exp", None, "seq"),
        P("exp", None),
        P(),
    )
    out_specs = (P("exp", "seq"), P("exp", "seq", None))
    return jax.shard_map(local, mesh=mesh, in_specs=in_specs, out_specs=out_specs, check_vma=False)
```
